32 devices in a mesh: fault: 16 (over z, x, core), rup: 2 (over y).
Axes of the slice: x: 2, y: 2, z: 4, core: 2. Of those that a mesh axis runs over, the one named last changes fastest.
Arguments:
- green: bfloat16 [32, 128, 6, 2, 2, 1024], P('fault', None, None, None, None, 'rup'), may hold values from -6 to 6
- slip_weights: bfloat16 [256, 16, 128, 6], P(('fault', 'rup')), may hold values from -0.0546875 to 0.0546875
- slip_spectra: bfloat16 [256, 16, 2, 1024], P(('fault', 'rup')), may hold values from -6 to 6
- block_lists: int32 [256, 16], P(('fault', 'rup')), may hold values from 0 to 31, all different within a row; in each aligned block of 16 rows (0 to 15, 16 to 31, ...) at most 12 rows name the same one
- block_counts: int32 [256], P(('fault', 'rup')), may hold values from 1 to 16, 3072 in all
- natural_freq: float32 [64], replicated, may hold values from 0.02 to 0.8
- damping: float32 [64], replicated, may hold values from 0.03 to 0.3
Outputs:
- waveforms: float32 [256, 2, 2048], P(('fault', 'rup'))
- osc_spectra: float32 [256, 2, 64], P(('fault', 'rup'))
The draws below stay inside these ranges and needn't reach their ends.
Inputs may be any that keep to these rules, and one draw needn't show every extreme that they name: `block_lists`: the 16 blocks of one rupture are distinct. In each aligned run of 16 ruptures no block is named by more than 12 slots, active or not, and some block is named by exactly 12. `block_counts`: the counts of all ruptures sum to 3072; some rupture has 16.
All inputs are finite; a program needn't handle non-finite values. No bound on the sum of `block_counts` on one device may be relied on, other than what follows from the above.
Results may differ from the reference program's by a relative error of at most 0.0037.
Values may be sent and summed in bfloat16 or wider, within the bound.
A program may use at most 64 MiB of HBM per device.

```python
import math
import jax
import jax.numpy as jnp
import numpy as np
from jax import lax

F = 1024
BLK_PTS = 128
TERMS = 6
COMPS = 2
PERIODS = 64
K = 16
RUP_DEV = 8
GROUP = 16
RUPTURES = 256
BLOCKS = 32
CAP = 12


def steps_of(stream_key, dims, split, least, high):
    factor_of = 1.0
    for position, shards_of in split:
        heights = jax.random.uniform(jax.random.fold_in(jax.random.fold_in(stream_key, 6), position), (shards_of,), jnp.float32, least / len(split), high / len(split))
        factor_of = factor_of * jnp.repeat(jnp.exp(heights), dims[position] // shards_of).reshape((-1,) + (1,) * (len(dims) - 1 - position))
    return factor_of


def split_up(count, total, limit, slope):
    portions = [(1 << 20) // math.isqrt(rank ** slope) + 1 for rank in range(2, count + 1)]
    spare, holding = total - limit - (count - 1), [1] * (count - 1)
    while spare > 0:
        movable = [i for i in range(count - 1) if holding[i] < limit]
        pool, left = sum([portions[i] for i in movable]), spare
        for i in movable:
            addition = min(limit - holding[i], max(1, left * portions[i] // pool), spare)
            holding[i] = holding[i] + addition
            spare = spare - addition
    return np.array([limit] + holding)


def uneven_parts(key, amount, total, bound, slope):
    if amount == 2:
        one = jax.random.randint(key, (), max(1, total - bound), min(bound, total - 1) + 1)
        return jnp.stack([one, total - one])
    sizes = jnp.asarray(split_up(amount, total, bound, slope), jnp.int32)
    twos = (amount - 1) // 2
    source_of, sink = sizes[1:1 + 2 * twos:2], sizes[2:2 + 2 * twos:2]
    room = jnp.minimum(source_of - 1, bound - sink)
    passed = jax.random.randint(jax.random.fold_in(key, 1), (twos,), 0, 1 << 20) % (room + 1)
    sizes = sizes.at[1:1 + 2 * twos:2].set(source_of - passed).at[2:2 + 2 * twos:2].set(sink + passed)
    return sizes[jax.random.permutation(jax.random.fold_in(key, 2), amount)]


def shared_out(rng, own, number, rows, count, top, limit, skew):
    order = jax.random.permutation(rng, count)
    crowded, common = shares(count, rows * top, limit, skew, True), shares(count, rows * top, limit, skew, False)
    places = jnp.arange(count)

    def named(lengths, offset_by):
        used = int((lengths > 0).sum())
        fixed = max(1, used // 4)
        shifted = fixed + (places - fixed + offset_by * (used - fixed)) % max(1, count - fixed)
        return jnp.zeros((count,), jnp.int32).at[order[jnp.where(places < fixed, places, shifted)]].set(jnp.asarray(lengths, jnp.int32))

    lengths = jnp.where(number % 4 == 0, named(crowded, number // 4), named(common, number - number // 4 - 1))
    mixed = jax.random.permutation(jax.random.fold_in(own, 3), count)
    donor, sink = mixed[0:count // 2 * 2:2], mixed[1:count // 2 * 2:2]
    margin = jnp.minimum(lengths[donor] - 1, limit - lengths[sink]) // 2
    margin = jnp.where((donor == order[0]) | (sink == order[0]) | (lengths[sink] == 0), 0, jnp.maximum(margin, 0))
    shifted = jax.random.randint(jax.random.fold_in(own, 4), (count // 2,), 0, 1 << 20) % (margin + 1)
    lengths = lengths.at[donor].add(-shifted).at[sink].add(shifted)
    members = jnp.searchsorted(jnp.cumsum(lengths), jnp.arange(rows * top), side="right").astype(jnp.int32)
    grid = members.reshape(top, rows).T
    grid = grid[jax.random.permutation(jax.random.fold_in(own, 1), rows)]
    offset_by = jax.random.randint(jax.random.fold_in(own, 2), (rows, 1), 0, top)
    return jnp.take_along_axis(grid, (jnp.arange(top)[None, :] + offset_by) % top, axis=1)


def shares(amount, total, reach, lean, full):
    weights = [(1 << 20) // math.isqrt(grade ** lean) + 1 for grade in range(1, amount + 1)]
    largest = reach if full else min(reach, max(-(-total // amount), total * weights[0] // sum(weights)))
    least = 1 if total - largest >= amount - 1 else 0
    counts, rest = [largest] + [least] * (amount - 1), total - largest - least * (amount - 1)
    while rest > 0:
        candidates = [i for i in range(1, amount) if counts[i] < largest] or [i for i in range(1, amount) if counts[i] < reach]
        pool, budget = sum([weights[i] for i in candidates]), rest
        for i in candidates:
            addition = min(reach - counts[i], max(1, budget * weights[i] // pool), rest)
            counts[i] = counts[i] + addition
            rest = rest - addition
    return np.array(counts)


def normal_values(stream_key, dims, scale, most, cuts=(), held_as=jnp.bfloat16):
    level = steps_of(stream_key, dims, cuts, -0.22, 0.18) if cuts else 1.0
    entries = jax.random.normal(stream_key, dims, jnp.float32) * scale * level
    return jnp.minimum(jnp.maximum(entries, -most), most).astype(held_as)


def setup_inputs(seed: int = 0) -> dict:
    key_of = jax.random.split(jax.random.key(seed), 8)
    green = normal_values(key_of[0], (BLOCKS, BLK_PTS, TERMS, COMPS, 2, F), 1.0, 6.0, ((0, 16), (5, 2)))
    slip_weights = normal_values(key_of[1], (RUPTURES, K, BLK_PTS, TERMS), (BLK_PTS * TERMS * K) ** -0.5, 0.0546875, ((0, 32),))
    slip_spectra = normal_values(key_of[2], (RUPTURES, K, 2, F), 0.7, 6.0, ((0, 32),))
    block_lists_keys = jax.random.split(jax.random.fold_in(key_of[3], 1), RUPTURES // GROUP)
    block_lists_turns = jax.random.permutation(jax.random.fold_in(key_of[3], 3), RUPTURES // GROUP)
    block_lists = jax.vmap(lambda own, number: shared_out(jax.random.fold_in(key_of[3], 2), own, number, GROUP, BLOCKS, K, CAP, 2))(block_lists_keys, block_lists_turns).reshape((RUPTURES, K))
    block_counts = uneven_parts(key_of[4], RUPTURES, 3 * RUPTURES * K // 4, K, 1).astype(jnp.int32)
    natural_freq = jnp.clip(jnp.exp(jax.random.uniform(key_of[5], (PERIODS,), jnp.float32, math.log(0.02), math.log(0.8))), 0.02, 0.8)
    damping = jnp.clip(jnp.exp(jax.random.uniform(key_of[6], (PERIODS,), jnp.float32, math.log(0.03), math.log(0.3))), 0.03, 0.3)
    return dict(green=green, slip_weights=slip_weights, slip_spectra=slip_spectra, block_lists=block_lists, block_counts=block_counts, natural_freq=natural_freq, damping=damping)


def inverse_table(freq_count):
    sample_count = 2 * freq_count
    freq_index = jnp.arange(freq_count, dtype=jnp.int32)
    time_index = jnp.arange(sample_count, dtype=jnp.int32)
    phase_index = freq_index[:, None] * time_index[None, :] % sample_count
    phase_angle = phase_index.astype(jnp.float32) * jnp.float32(2.0 * math.pi / sample_count)
    norm_scale = jnp.float32(1.0 / math.sqrt(freq_count))
    cosines = jnp.cos(phase_angle) * norm_scale
    sines = -jnp.sin(phase_angle) * norm_scale
    return jnp.concatenate([cosines, sines], axis=0).astype(jnp.bfloat16)

def oscillator_gain(natural_freq, damping, freq_count):
    omega_f = jnp.arange(freq_count, dtype=jnp.float32) * jnp.float32(math.pi / freq_count)
    omega_nat = jnp.float32(math.pi) * natural_freq[:, None]
    stiffness = omega_nat * omega_nat
    den_real = stiffness - omega_f[None, :] * omega_f[None, :]
    den_imag = 2.0 * damping[:, None] * omega_nat * omega_f[None, :]
    magnitude = den_real * den_real + den_imag * den_imag
    return (stiffness * den_real / magnitude, -stiffness * den_imag / magnitude)

def oscillate(spectra, gain_real, gain_imag, dft_table):
    rupture_count = spectra.shape[0]
    comp_count = spectra.shape[1]
    freq_count = spectra.shape[3]
    period_count = gain_real.shape[0]
    spec_real = spectra[:, :, 0][:, :, None, :]
    spec_imag = spectra[:, :, 1][:, :, None, :]
    resp_real = gain_real * spec_real - gain_imag * spec_imag
    resp_imag = gain_real * spec_imag + gain_imag * spec_real
    resp_rows = jnp.concatenate([resp_real, resp_imag], axis=3).astype(jnp.bfloat16)
    resp_rows = resp_rows.reshape(rupture_count * comp_count * period_count, 2 * freq_count)
    wave_rows = spectra.reshape(rupture_count * comp_count, 2 * freq_count).astype(jnp.bfloat16)
    stacked = jnp.concatenate([resp_rows, wave_rows], axis=0)
    outcome = jnp.dot(stacked, dft_table, preferred_element_type=jnp.float32)
    split_at = rupture_count * comp_count * period_count
    peaks = lax.optimization_barrier(jnp.max(jnp.abs(outcome[:split_at]), axis=1)).reshape(rupture_count, comp_count, period_count)
    waveform = outcome[split_at:].reshape(rupture_count, comp_count, 2 * freq_count)
    return (waveform, peaks)

def reference(green, slip_weights, slip_spectra, block_lists, block_counts, natural_freq, damping):
    inner_width = BLK_PTS * TERMS
    tile_mats = green.reshape(BLOCKS, inner_width, COMPS, 2, F)

    def per_rupture(record):
        weights, slip, chosen, active_count = record
        picked = tile_mats[chosen].astype(jnp.float32)
        product = jnp.einsum('ki,kicef->kcef', weights.reshape(K, inner_width).astype(jnp.float32), picked)
        slip_f = slip.astype(jnp.float32)
        slip_real = slip_f[:, 0][:, None, :]
        slip_imag = slip_f[:, 1][:, None, :]
        real_part = product[:, :, 0] * slip_real - product[:, :, 1] * slip_imag
        imag_part = product[:, :, 0] * slip_imag + product[:, :, 1] * slip_real
        active = jnp.arange(K, dtype=jnp.int32) < active_count
        term_rows = jnp.where(active[:, None, None, None], jnp.stack([real_part, imag_part], axis=2), jnp.float32(0.0))
        return lax.optimization_barrier(jnp.sum(term_rows, axis=0))
    spectra = lax.map(per_rupture, (slip_weights, slip_spectra, block_lists, block_counts))
    gain_real, gain_imag = oscillator_gain(natural_freq, damping, F)
    dft_table = inverse_table(F)
    grouped = spectra.reshape(RUPTURES // RUP_DEV, RUP_DEV, COMPS, 2, F)

    def per_group(spec_group):
        return oscillate(spec_group, gain_real, gain_imag, dft_table)
    waveform, peaks = lax.map(per_group, grouped)
    return (waveform.reshape(RUPTURES, COMPS, 2 * F), peaks.reshape(RUPTURES, COMPS, PERIODS))
```

```python
import math

import jax
import jax.numpy as jnp
from jax import lax
from jax.sharding import PartitionSpec as P


def inverse_table(freq_count):
    sample_count = 2 * freq_count
    freq_index = jnp.arange(freq_count, dtype=jnp.int32)
    time_index = jnp.arange(sample_count, dtype=jnp.int32)
    phase_index = freq_index[:, None] * time_index[None, :] % sample_count
    phase_angle = phase_index.astype(jnp.float32) * jnp.float32(2.0 * math.pi / sample_count)
    norm_scale = jnp.float32(1.0 / math.sqrt(freq_count))
    cosines = jnp.cos(phase_angle) * norm_scale
    sines = -jnp.sin(phase_angle) * norm_scale
    return jnp.concatenate([cosines, sines], axis=0).astype(jnp.bfloat16)


def oscillator_gain(natural_freq, damping, freq_count):
    omega_f = jnp.arange(freq_count, dtype=jnp.float32) * jnp.float32(math.pi / freq_count)
    omega_nat = jnp.float32(math.pi) * natural_freq[:, None]
    stiffness = omega_nat * omega_nat
    den_real = stiffness - omega_f[None, :] * omega_f[None, :]
    den_imag = 2.0 * damping[:, None] * omega_nat * omega_f[None, :]
    magnitude = den_real * den_real + den_imag * den_imag
    return (stiffness * den_real / magnitude, -stiffness * den_imag / magnitude)


def oscillate(spectra, gain_real, gain_imag, dft_table):
    rupture_count = spectra.shape[0]
    comp_count = spectra.shape[1]
    freq_count = spectra.shape[3]
    period_count = gain_real.shape[0]
    spec_real = spectra[:, :, 0][:, :, None, :]
    spec_imag = spectra[:, :, 1][:, :, None, :]
    resp_real = gain_real * spec_real - gain_imag * spec_imag
    resp_imag = gain_real * spec_imag + gain_imag * spec_real
    resp_rows = jnp.concatenate([resp_real, resp_imag], axis=3).astype(jnp.bfloat16)
    resp_rows = resp_rows.reshape(rupture_count * comp_count * period_count, 2 * freq_count)
    wave_rows = spectra.reshape(rupture_count * comp_count, 2 * freq_count).astype(jnp.bfloat16)
    stacked = jnp.concatenate([resp_rows, wave_rows], axis=0)
    outcome = jnp.dot(stacked, dft_table, preferred_element_type=jnp.float32)
    split_at = rupture_count * comp_count * period_count
    peaks = jnp.max(jnp.abs(outcome[:split_at]), axis=1).reshape(
        rupture_count, comp_count, period_count
    )
    waveform = outcome[split_at:].reshape(rupture_count, comp_count, 2 * freq_count)
    return (waveform, peaks)


def body(green, slip_weights, slip_spectra, block_lists, block_counts, natural_freq, damping):
    fault_count = lax.axis_size("fault")
    group_size = lax.axis_size("rup")
    owned_count, slot_width = block_lists.shape
    blocks_local, points, terms, comp_count, _, freq_local = green.shape
    freq_count = slip_spectra.shape[3]
    inner_width = points * terms
    block_total = blocks_local * fault_count
    device_count = fault_count * group_size
    slot_rows = owned_count * slot_width
    axes = ("fault", "rup")
    slot_index = lax.broadcasted_iota(jnp.int32, (owned_count, slot_width), 1)
    named = jnp.where(slot_index < block_counts[:, None], block_lists, -1).reshape(1, slot_rows)
    pick_shape = (block_total, owned_count, slot_rows)
    row_block = lax.broadcasted_iota(jnp.int32, pick_shape, 0)
    row_owner = lax.broadcasted_iota(jnp.int32, pick_shape, 1)
    col_owner = lax.broadcasted_iota(jnp.int32, pick_shape, 2) // slot_width
    pick = ((named[None] == row_block) & (row_owner == col_owner)).astype(jnp.bfloat16)
    pick = pick.reshape(block_total * owned_count, slot_rows)
    weight_rows = slip_weights.transpose(0, 1, 3, 2).reshape(slot_rows, inner_width)
    weight_send = jnp.dot(pick, weight_rows, preferred_element_type=jnp.float32).astype(jnp.bfloat16)
    weight_send = jnp.broadcast_to(
        weight_send.reshape(fault_count, 1, blocks_local, owned_count, inner_width),
        (fault_count, group_size, blocks_local, owned_count, inner_width),
    ).reshape(device_count, blocks_local, owned_count, inner_width)
    weight_recv = lax.all_to_all(weight_send, axes, split_axis=0, concat_axis=0, tiled=True)
    slip_rows = slip_spectra.reshape(slot_rows, 2, group_size, freq_local).transpose(0, 2, 1, 3)
    slip_rows = slip_rows.reshape(slot_rows, 2 * freq_count)
    slip_send = jnp.dot(pick, slip_rows, preferred_element_type=jnp.float32).astype(jnp.bfloat16)
    slip_send = slip_send.reshape(
        fault_count, blocks_local, owned_count, group_size, 2, freq_local
    ).transpose(0, 3, 1, 4, 2, 5)
    slip_send = slip_send.reshape(device_count, blocks_local, 2, owned_count, freq_local)
    slip_recv = lax.all_to_all(slip_send, axes, split_axis=0, concat_axis=0, tiled=True)
    tile_mats = green.transpose(0, 2, 1, 3, 4, 5).reshape(
        blocks_local, inner_width, comp_count * 2 * freq_local
    )
    total_real, total_imag = 0.0, 0.0
    for b in range(blocks_local):
        rows = weight_recv[:, b].reshape(device_count * owned_count, inner_width)
        product = jnp.dot(rows, tile_mats[b], preferred_element_type=jnp.float32)
        product = product.reshape(device_count, owned_count, comp_count, 2, freq_local)
        slip_f = slip_recv[:, b].astype(jnp.float32)
        slip_real = slip_f[:, 0][:, :, None]
        slip_imag = slip_f[:, 1][:, :, None]
        prod_real, prod_imag = product[:, :, :, 0], product[:, :, :, 1]
        total_real = total_real + prod_real * slip_real - prod_imag * slip_imag
        total_imag = total_imag + prod_real * slip_imag + prod_imag * slip_real
    partial = jnp.stack([total_real, total_imag], axis=1).astype(jnp.bfloat16)
    partial = partial.transpose(0, 3, 1, 2, 4)
    returned = lax.all_to_all(partial, axes, split_axis=0, concat_axis=0, tiled=True)
    returned = returned.reshape(
        fault_count, group_size, comp_count, 2, owned_count, freq_local
    ).astype(jnp.float32)
    spectra = jnp.sum(returned, axis=0).transpose(3, 1, 2, 0, 4)
    spectra = spectra.reshape(owned_count, comp_count, 2, freq_count)
    gain_real, gain_imag = oscillator_gain(natural_freq, damping, freq_count)
    dft_table = inverse_table(freq_count)
    waveform, peaks = oscillate(spectra, gain_real, gain_imag, dft_table)
    return (waveform, peaks)


def solution(mesh):
    return jax.shard_map(
        body,
        mesh=mesh,
        in_specs=(
            P("fault", None, None, None, None, "rup"),
            P(("fault", "rup"), None, None, None),
            P(("fault", "rup"), None, None, None),
            P(("fault", "rup"), None),
            P(("fault", "rup")),
            P(),
            P(),
        ),
        out_specs=(P(("fault", "rup"), None, None), P(("fault", "rup"), None, None)),
        check_vma=False,
    )
```

```python
import math

import jax
import jax.numpy as jnp
from jax import lax
from jax.experimental import pallas as pl
from jax.experimental.pallas import tpu as pltpu
from jax.sharding import PartitionSpec as P

LANES = 128


def phase_waves(freq_index, time_index, sample_count):
    phase = freq_index[:, None] * time_index[None, :] % sample_count
    angle = phase.astype(jnp.float32) * jnp.float32(2.0 * math.pi / sample_count)
    return jnp.cos(angle), jnp.sin(angle)


def half_tables(freq_count):
    sample_count = 2 * freq_count
    scale = jnp.float32(1.0 / math.sqrt(freq_count))
    fine = jnp.arange(LANES, dtype=jnp.int32)
    coarse = jnp.arange(freq_count // LANES, dtype=jnp.int32) * LANES
    cosines, sines = [], []
    for parity in range(2):
        freq_index = 2 * jnp.arange(freq_count // 2, dtype=jnp.int32) + parity
        cos_f, sin_f = phase_waves(freq_index, fine, sample_count)
        cos_c, sin_c = phase_waves(freq_index, coarse, sample_count)
        cos_f, sin_f, cos_c, sin_c = lax.optimization_barrier(
            (cos_f * scale, sin_f * scale, cos_c, sin_c)
        )
        cos_parts, sin_parts = [], []
        for a in range(freq_count // LANES):
            ca, sa = cos_c[:, a : a + 1], sin_c[:, a : a + 1]
            cos_parts.append((ca * cos_f - sa * sin_f).astype(jnp.bfloat16))
            sin_parts.append((-(sa * cos_f + ca * sin_f)).astype(jnp.bfloat16))
        cosines.append(jnp.concatenate(cos_parts, axis=1))
        sines.append(jnp.concatenate(sin_parts, axis=1))
    return (cosines[0], cosines[1], sines[0], sines[1])


def split_gain(natural_freq, damping, freq_count):
    freq_index = jnp.arange(freq_count, dtype=jnp.float32).reshape(freq_count // 2, 2).T
    freq_index = freq_index.reshape(1, 2, 1, freq_count // 2)
    omega_f = freq_index * jnp.float32(math.pi / freq_count)
    omega_nat = (jnp.float32(math.pi) * natural_freq)[None, None, :, None]
    stiffness = omega_nat * omega_nat
    den_real = stiffness - omega_f * omega_f
    den_imag = 2.0 * damping[None, None, :, None] * omega_nat * omega_f
    magnitude = den_real * den_real + den_imag * den_imag
    return jnp.concatenate(
        [stiffness * den_real / magnitude, -stiffness * den_imag / magnitude], axis=0
    )


def oscillate_kernel(spec_ref, gain_ref, ce_ref, co_ref, se_ref, so_ref, wave_ref, peak_ref):
    step = pl.program_id(0)
    rows_per = peak_ref.shape[1]
    period_count, half = gain_ref.shape[2], gain_ref.shape[3]
    f32 = jnp.float32
    tables = (ce_ref, co_ref, se_ref, so_ref)

    @pl.when(step == 0)
    def _():
        parts = [
            jnp.dot(spec_ref[i // 2, i % 2].astype(jnp.bfloat16), tables[i][...], preferred_element_type=f32)
            for i in range(4)
        ]
        even, odd = parts[0] + parts[2], parts[1] + parts[3]
        wave_ref[:, : 2 * half] = even + odd
        wave_ref[:, 2 * half :] = even - odd

    stacked = [[], [], [], []]
    for r in range(rows_per):
        row = pl.ds(step * rows_per + r, 1)
        for parity in range(2):
            sr, si = spec_ref[0, parity, row, :], spec_ref[1, parity, row, :]
            gr, gi = gain_ref[0, parity], gain_ref[1, parity]
            stacked[parity].append((gr * sr - gi * si).astype(jnp.bfloat16))
            stacked[2 + parity].append((gr * si + gi * sr).astype(jnp.bfloat16))
    rows = [jnp.concatenate(group, axis=0) for group in stacked]
    ce, co, se, so = (
        jnp.dot(rows[i], tables[i][:, :half], preferred_element_type=f32) for i in range(4)
    )
    best = jnp.maximum(
        jnp.abs(ce + co) + jnp.abs(se + so), jnp.abs(ce - co) + jnp.abs(se - so)
    )
    best = jnp.max(best, axis=1, keepdims=True)
    lane = lax.broadcasted_iota(jnp.int32, (1, half), 1)
    signs = jnp.where(lane % 2 == 0, f32(1.0), f32(-1.0)) * f32(1.0 / math.sqrt(2 * half))
    middle = jnp.abs(jnp.sum(rows[0].astype(f32) * signs, axis=1, keepdims=True)) + jnp.abs(
        jnp.sum(rows[3].astype(f32) * signs, axis=1, keepdims=True)
    )
    best = jnp.maximum(best, middle)
    shape = (period_count, period_count)
    diag = lax.broadcasted_iota(jnp.int32, shape, 0) == lax.broadcasted_iota(jnp.int32, shape, 1)
    for r in range(rows_per):
        column = best[r * period_count : (r + 1) * period_count]
        peak_ref[0, r : r + 1, :] = jnp.sum(
            jnp.where(diag, column, f32(0.0)), axis=0, keepdims=True
        )


def oscillate(spectra, gain, tables):
    row_count, half = spectra.shape[2:]
    period_count = gain.shape[2]
    rows_per = math.gcd(row_count, 4)
    steps = row_count // rows_per
    whole = lambda shape: pl.BlockSpec(shape, lambda i: (0,) * len(shape), pipeline_mode=pl.Buffered(1))
    wave, peak = pl.pallas_call(
        oscillate_kernel,
        grid=(steps,),
        in_specs=[whole(spectra.shape), whole(gain.shape)] + [whole(t.shape) for t in tables],
        out_specs=[
            pl.BlockSpec((row_count, 4 * half), lambda i: (0, 0)),
            pl.BlockSpec((1, rows_per, period_count), lambda i: (i, 0, 0)),
        ],
        out_shape=[
            jax.ShapeDtypeStruct((row_count, 4 * half), jnp.float32),
            jax.ShapeDtypeStruct((steps, rows_per, period_count), jnp.float32),
        ],
        compiler_params=pltpu.CompilerParams(vmem_limit_bytes=40 << 20),
    )(spectra, gain, *tables)
    return wave, peak


def body(green, slip_weights, slip_spectra, block_lists, block_counts, natural_freq, damping):
    fault_count = lax.axis_size("fault")
    group_size = lax.axis_size("rup")
    owned_count, slot_width = block_lists.shape
    blocks_local, points, terms, comp_count, _, freq_local = green.shape
    freq_count = slip_spectra.shape[3]
    inner_width = points * terms
    block_total = blocks_local * fault_count
    device_count = fault_count * group_size
    slot_rows = owned_count * slot_width
    axes = ("fault", "rup")
    bf16, f32 = jnp.bfloat16, jnp.float32
    slot_index = lax.broadcasted_iota(jnp.int32, (owned_count, slot_width), 1)
    named = jnp.where(slot_index < block_counts[:, None], block_lists, -1).reshape(1, slot_rows)
    pick_shape = (block_total, owned_count, slot_rows)
    row_block = lax.broadcasted_iota(jnp.int32, pick_shape, 0)
    row_owner = lax.broadcasted_iota(jnp.int32, pick_shape, 1)
    col_owner = lax.broadcasted_iota(jnp.int32, pick_shape, 2) // slot_width
    pick = ((named[None] == row_block) & (row_owner == col_owner)).astype(bf16)
    pick = pick.reshape(block_total * owned_count, slot_rows)
    from_index = jnp.arange(inner_width, dtype=jnp.int32)
    to_index = (from_index % points) * terms + from_index // points
    turn = (to_index[:, None] == from_index[None, :]).astype(bf16)
    weight_rows = slip_weights.transpose(0, 1, 3, 2).reshape(slot_rows, inner_width)
    weight_rows = jnp.dot(weight_rows, turn, preferred_element_type=f32).astype(bf16)
    weight_send = jnp.dot(pick, weight_rows, preferred_element_type=f32).astype(bf16)
    weight_send = jnp.broadcast_to(
        weight_send.reshape(fault_count, 1, blocks_local, owned_count, inner_width),
        (fault_count, group_size, blocks_local, owned_count, inner_width),
    ).reshape(device_count, blocks_local, owned_count, inner_width)
    weight_recv = lax.all_to_all(weight_send, axes, split_axis=0, concat_axis=0, tiled=True)
    slip_rows = slip_spectra.reshape(slot_rows, 2, group_size, freq_local).transpose(0, 2, 1, 3)
    slip_rows = slip_rows.reshape(slot_rows, 2 * freq_count)
    slip_send = jnp.dot(pick, slip_rows, preferred_element_type=f32).astype(bf16)
    slip_send = slip_send.reshape(
        fault_count, blocks_local, owned_count, group_size, 2, freq_local
    ).transpose(0, 3, 1, 4, 2, 5)
    slip_send = slip_send.reshape(device_count, blocks_local, 2, owned_count, freq_local)
    slip_recv = lax.all_to_all(slip_send, axes, split_axis=0, concat_axis=0, tiled=True)
    tile_mats = green.reshape(blocks_local, inner_width, comp_count * 2 * freq_local)
    product = jnp.einsum("sbqi,bix->sbqx", weight_recv, tile_mats, preferred_element_type=f32)
    slip_f = slip_recv.astype(f32)
    ones = []
    for c in range(comp_count):
        at = 2 * c * freq_local
        prod_real = product[:, :, :, at : at + freq_local]
        prod_imag = product[:, :, :, at + freq_local : at + 2 * freq_local]
        slip_real, slip_imag = slip_f[:, :, 0], slip_f[:, :, 1]
        ones.append(jnp.sum(prod_real * slip_real - prod_imag * slip_imag, axis=1))
        ones.append(jnp.sum(prod_real * slip_imag + prod_imag * slip_real, axis=1))
    partial = jnp.stack([one.astype(bf16) for one in ones], axis=1)
    order = jnp.arange(freq_local, dtype=jnp.int32)
    split_to = (order % 2) * (freq_local // 2) + order // 2
    deal = (split_to[:, None] == order[None, :]).astype(bf16)
    partial = jnp.dot(
        partial.reshape(device_count * comp_count * 2 * owned_count, freq_local),
        deal,
        preferred_element_type=f32,
    ).astype(bf16)
    partial = partial.reshape(device_count, comp_count * 2, owned_count, freq_local)
    returned = lax.all_to_all(partial, axes, split_axis=0, concat_axis=0, tiled=True)
    returned = returned.reshape(
        fault_count, group_size, comp_count, 2, owned_count, 2, freq_local // 2
    ).astype(f32)
    spectra = jnp.sum(returned, axis=0).transpose(2, 4, 1, 3, 0, 5)
    spectra = spectra.reshape(2, 2, comp_count * owned_count, freq_count // 2)
    gain = split_gain(natural_freq, damping, freq_count)
    tables = half_tables(freq_count)
    wave, peak = oscillate(spectra, gain, tables)
    period_count = natural_freq.shape[0]
    waveform = wave.reshape(comp_count, owned_count, 2 * freq_count).transpose(1, 0, 2)
    peaks = peak.reshape(comp_count, owned_count, period_count).transpose(1, 0, 2)
    return (waveform, peaks)


def solution(mesh):
    return jax.shard_map(
        body,
        mesh=mesh,
        in_specs=(
            P("fault", None, None, None, None, "rup"),
            P(("fault", "rup"), None, None, None),
            P(("fault", "rup"), None, None, None),
            P(("fault", "rup"), None),
            P(("fault", "rup")),
            P(),
            P(),
        ),
        out_specs=(P(("fault", "rup"), None, None), P(("fault", "rup"), None, None)),
        check_vma=False,
    )
```

```python
import math

import jax
import jax.numpy as jnp
from jax import lax
from jax.experimental import pallas as pl
from jax.experimental.pallas import tpu as pltpu
from jax.sharding import PartitionSpec as P

LANES = 128


def phase_waves(freq_index, time_index, sample_count):
    phase = freq_index[:, None] * time_index[None, :] % sample_count
    angle = phase.astype(jnp.float32) * jnp.float32(2.0 * math.pi / sample_count)
    return jnp.cos(angle), jnp.sin(angle)


def half_tables(freq_count):
    sample_count = 2 * freq_count
    scale = jnp.float32(1.0 / math.sqrt(freq_count))
    fine = jnp.arange(LANES, dtype=jnp.int32)
    coarse = jnp.arange(freq_count // LANES, dtype=jnp.int32) * LANES
    cosines, sines = [], []
    for parity in range(2):
        freq_index = 2 * jnp.arange(freq_count // 2, dtype=jnp.int32) + parity
        cos_f, sin_f = phase_waves(freq_index, fine, sample_count)
        cos_c, sin_c = phase_waves(freq_index, coarse, sample_count)
        cos_f, sin_f, cos_c, sin_c = lax.optimization_barrier(
            (cos_f * scale, sin_f * scale, cos_c, sin_c)
        )
        cos_parts, sin_parts = [], []
        for a in range(freq_count // LANES):
            ca, sa = cos_c[:, a : a + 1], sin_c[:, a : a + 1]
            cos_parts.append((ca * cos_f - sa * sin_f).astype(jnp.bfloat16))
            sin_parts.append((-(sa * cos_f + ca * sin_f)).astype(jnp.bfloat16))
        cosines.append(jnp.concatenate(cos_parts, axis=1))
        sines.append(jnp.concatenate(sin_parts, axis=1))
    return (cosines[0], cosines[1], sines[0], sines[1])


def split_gain(natural_freq, damping, freq_count):
    freq_index = jnp.arange(freq_count, dtype=jnp.float32).reshape(freq_count // 2, 2).T
    freq_index = freq_index.reshape(1, 2, 1, freq_count // 2)
    omega_f = freq_index * jnp.float32(math.pi / freq_count)
    omega_nat = (jnp.float32(math.pi) * natural_freq)[None, None, :, None]
    stiffness = omega_nat * omega_nat
    den_real = stiffness - omega_f * omega_f
    den_imag = 2.0 * damping[None, None, :, None] * omega_nat * omega_f
    magnitude = den_real * den_real + den_imag * den_imag
    return jnp.concatenate(
        [stiffness * den_real / magnitude, -stiffness * den_imag / magnitude], axis=0
    )


def oscillate_kernel(spec_ref, gain_ref, ce_ref, co_ref, se_ref, so_ref, wave_ref, peak_ref):
    step = pl.program_id(0)
    rows_per = peak_ref.shape[1]
    period_count, half = gain_ref.shape[2], gain_ref.shape[3]
    f32 = jnp.float32
    tables = (ce_ref, co_ref, se_ref, so_ref)

    @pl.when(step == 0)
    def _():
        parts = [
            jnp.dot(spec_ref[i // 2, i % 2].astype(jnp.bfloat16), tables[i][...], preferred_element_type=f32)
            for i in range(4)
        ]
        even, odd = parts[0] + parts[2], parts[1] + parts[3]
        wave_ref[:, : 2 * half] = even + odd
        wave_ref[:, 2 * half :] = even - odd

    stacked = [[], [], [], []]
    for r in range(rows_per):
        row = pl.ds(step * rows_per + r, 1)
        for parity in range(2):
            sr, si = spec_ref[0, parity, row, :], spec_ref[1, parity, row, :]
            gr, gi = gain_ref[0, parity], gain_ref[1, parity]
            stacked[parity].append((gr * sr - gi * si).astype(jnp.bfloat16))
            stacked[2 + parity].append((gr * si + gi * sr).astype(jnp.bfloat16))
    rows = [jnp.concatenate(group, axis=0) for group in stacked]
    ce, co, se, so = (
        jnp.dot(rows[i], tables[i][:, :half], preferred_element_type=f32) for i in range(4)
    )
    best = jnp.maximum(
        jnp.abs(ce + co) + jnp.abs(se + so), jnp.abs(ce - co) + jnp.abs(se - so)
    )
    best = jnp.max(best, axis=1, keepdims=True)
    lane = lax.broadcasted_iota(jnp.int32, (1, half), 1)
    signs = jnp.where(lane % 2 == 0, f32(1.0), f32(-1.0)) * f32(1.0 / math.sqrt(2 * half))
    middle = jnp.abs(jnp.sum(rows[0].astype(f32) * signs, axis=1, keepdims=True)) + jnp.abs(
        jnp.sum(rows[3].astype(f32) * signs, axis=1, keepdims=True)
    )
    best = jnp.maximum(best, middle)
    shape = (period_count, period_count)
    diag = lax.broadcasted_iota(jnp.int32, shape, 0) == lax.broadcasted_iota(jnp.int32, shape, 1)
    for r in range(rows_per):
        column = best[r * period_count : (r + 1) * period_count]
        peak_ref[0, r : r + 1, :] = jnp.sum(
            jnp.where(diag, column, f32(0.0)), axis=0, keepdims=True
        )


def oscillate(spectra, gain, tables):
    row_count, half = spectra.shape[2:]
    period_count = gain.shape[2]
    rows_per = math.gcd(row_count, 4)
    steps = row_count // rows_per
    whole = lambda shape: pl.BlockSpec(shape, lambda i: (0,) * len(shape), pipeline_mode=pl.Buffered(1))
    wave, peak = pl.pallas_call(
        oscillate_kernel,
        grid=(steps,),
        in_specs=[whole(spectra.shape), whole(gain.shape)] + [whole(t.shape) for t in tables],
        out_specs=[
            pl.BlockSpec((row_count, 4 * half), lambda i: (0, 0)),
            pl.BlockSpec((1, rows_per, period_count), lambda i: (i, 0, 0)),
        ],
        out_shape=[
            jax.ShapeDtypeStruct((row_count, 4 * half), jnp.float32),
            jax.ShapeDtypeStruct((steps, rows_per, period_count), jnp.float32),
        ],
        compiler_params=pltpu.CompilerParams(vmem_limit_bytes=40 << 20),
    )(spectra, gain, *tables)
    return wave, peak


def body(green, slip_weights, slip_spectra, block_lists, block_counts, natural_freq, damping):
    fault_count = lax.axis_size("fault")
    group_size = lax.axis_size("rup")
    owned_count, slot_width = block_lists.shape
    blocks_local, points, terms, comp_count, _, freq_local = green.shape
    freq_count = slip_spectra.shape[3]
    inner_width = points * terms
    block_total = blocks_local * fault_count
    device_count = fault_count * group_size
    slot_rows = owned_count * slot_width
    axes = ("fault", "rup")
    bf16, f32 = jnp.bfloat16, jnp.float32
    slot_index = lax.broadcasted_iota(jnp.int32, (owned_count, slot_width), 1)
    named = jnp.where(slot_index < block_counts[:, None], block_lists, -1).reshape(1, slot_rows)
    pick_shape = (block_total, owned_count, slot_rows)
    row_block = lax.broadcasted_iota(jnp.int32, pick_shape, 0)
    row_owner = lax.broadcasted_iota(jnp.int32, pick_shape, 1)
    col_owner = lax.broadcasted_iota(jnp.int32, pick_shape, 2) // slot_width
    pick = ((named[None] == row_block) & (row_owner == col_owner)).astype(bf16)
    pick = pick.reshape(block_total * owned_count, slot_rows)
    from_index = jnp.arange(inner_width, dtype=jnp.int32)
    to_index = (from_index % points) * terms + from_index // points
    turn = (to_index[:, None] == from_index[None, :]).astype(bf16)
    weight_rows = slip_weights.transpose(0, 1, 3, 2).reshape(slot_rows, inner_width)
    weight_rows = jnp.dot(weight_rows, turn, preferred_element_type=f32).astype(bf16)
    weight_send = jnp.dot(pick, weight_rows, preferred_element_type=f32).astype(bf16)
    weight_send = weight_send.reshape(fault_count, blocks_local, owned_count, inner_width)
    weight_own = lax.all_to_all(weight_send, "fault", split_axis=0, concat_axis=0, tiled=True)
    rup = lax.axis_index("rup")
    weight_recv = [weight_own]
    for shift in range(1, group_size):
        ring = [(i, (i + shift) % group_size) for i in range(group_size)]
        weight_recv.append(lax.ppermute(weight_own, "rup", ring))
    slip_rows = slip_spectra.reshape(slot_rows, 2, group_size, freq_local).transpose(0, 2, 1, 3)
    slip_rows = slip_rows.reshape(slot_rows, 2 * freq_count)
    slip_send = jnp.dot(pick, slip_rows, preferred_element_type=f32).astype(bf16)
    slip_send = slip_send.reshape(
        fault_count, blocks_local, owned_count, group_size, 2, freq_local
    ).transpose(0, 3, 1, 4, 2, 5)
    slip_send = slip_send.reshape(device_count, blocks_local, 2, owned_count, freq_local)
    slip_recv = lax.all_to_all(slip_send, axes, split_axis=0, concat_axis=0, tiled=True)
    tile_mats = green.reshape(blocks_local, inner_width, comp_count * 2 * freq_local)
    weight_all = jnp.stack(
        [
            lax.select_n((rup - g) % group_size, *weight_recv)
            if group_size == 2
            else lax.dynamic_index_in_dim(
                jnp.stack(weight_recv), (rup - g) % group_size, 0, keepdims=False
            )
            for g in range(group_size)
        ],
        axis=1,
    ).reshape(device_count, blocks_local, owned_count, inner_width)
    product = jnp.einsum("sbqi,bix->sbqx", weight_all, tile_mats, preferred_element_type=f32)
    slip_f = slip_recv.astype(f32)
    ones = []
    for c in range(comp_count):
        at = 2 * c * freq_local
        prod_real = product[:, :, :, at : at + freq_local]
        prod_imag = product[:, :, :, at + freq_local : at + 2 * freq_local]
        slip_real, slip_imag = slip_f[:, :, 0], slip_f[:, :, 1]
        ones.append(jnp.sum(prod_real * slip_real - prod_imag * slip_imag, axis=1))
        ones.append(jnp.sum(prod_real * slip_imag + prod_imag * slip_real, axis=1))
    partial = jnp.stack([one.astype(bf16) for one in ones], axis=1)
    order = jnp.arange(freq_local, dtype=jnp.int32)
    split_to = (order % 2) * (freq_local // 2) + order // 2
    deal = (split_to[:, None] == order[None, :]).astype(bf16)
    partial = jnp.dot(
        partial.reshape(device_count * comp_count * 2 * owned_count, freq_local),
        deal,
        preferred_element_type=f32,
    ).astype(bf16)
    partial = partial.reshape(device_count, comp_count * 2, owned_count, freq_local)
    returned = lax.all_to_all(partial, axes, split_axis=0, concat_axis=0, tiled=True)
    returned = returned.reshape(
        fault_count, group_size, comp_count, 2, owned_count, 2, freq_local // 2
    ).astype(f32)
    spectra = jnp.sum(returned, axis=0).transpose(2, 4, 1, 3, 0, 5)
    spectra = spectra.reshape(2, 2, comp_count * owned_count, freq_count // 2)
    gain = split_gain(natural_freq, damping, freq_count)
    tables = half_tables(freq_count)
    wave, peak = oscillate(spectra, gain, tables)
    period_count = natural_freq.shape[0]
    waveform = wave.reshape(comp_count, owned_count, 2 * freq_count).transpose(1, 0, 2)
    peaks = peak.reshape(comp_count, owned_count, period_count).transpose(1, 0, 2)
    return (waveform, peaks)


def solution(mesh):
    return jax.shard_map(
        body,
        mesh=mesh,
        in_specs=(
            P("fault", None, None, None, None, "rup"),
            P(("fault", "rup"), None, None, None),
            P(("fault", "rup"), None, None, None),
            P(("fault", "rup"), None),
            P(("fault", "rup")),
            P(),
            P(),
        ),
        out_specs=(P(("fault", "rup"), None, None), P(("fault", "rup"), None, None)),
        check_vma=False,
    )
```

```python
import math

import jax
import jax.numpy as jnp
from jax import lax
from jax.experimental import pallas as pl
from jax.experimental.pallas import tpu as pltpu
from jax.sharding import PartitionSpec as P

LANES = 128


def phase_waves(freq_index, time_index, sample_count):
    phase = freq_index[:, None] * time_index[None, :] % sample_count
    angle = phase.astype(jnp.float32) * jnp.float32(2.0 * math.pi / sample_count)
    return jnp.cos(angle), jnp.sin(angle)


def half_tables(freq_count):
    sample_count = 2 * freq_count
    scale = jnp.float32(1.0 / math.sqrt(freq_count))
    fine = jnp.arange(LANES, dtype=jnp.int32)
    coarse = jnp.arange(freq_count // LANES, dtype=jnp.int32) * LANES
    cosines, sines = [], []
    for parity in range(2):
        freq_index = 2 * jnp.arange(freq_count // 2, dtype=jnp.int32) + parity
        cos_f, sin_f = phase_waves(freq_index, fine, sample_count)
        cos_c, sin_c = phase_waves(freq_index, coarse, sample_count)
        cos_f, sin_f, cos_c, sin_c = lax.optimization_barrier(
            (cos_f * scale, sin_f * scale, cos_c, sin_c)
        )
        cos_parts, sin_parts = [], []
        for a in range(freq_count // LANES):
            ca, sa = cos_c[:, a : a + 1], sin_c[:, a : a + 1]
            cos_parts.append((ca * cos_f - sa * sin_f).astype(jnp.bfloat16))
            sin_parts.append((-(sa * cos_f + ca * sin_f)).astype(jnp.bfloat16))
        cosines.append(jnp.concatenate(cos_parts, axis=1))
        sines.append(jnp.concatenate(sin_parts, axis=1))
    return (cosines[0], cosines[1], sines[0], sines[1])


def split_gain(natural_freq, damping, freq_count):
    freq_index = jnp.arange(freq_count, dtype=jnp.float32).reshape(freq_count // 2, 2).T
    freq_index = freq_index.reshape(1, 2, 1, freq_count // 2)
    omega_f = freq_index * jnp.float32(math.pi / freq_count)
    omega_nat = (jnp.float32(math.pi) * natural_freq)[None, None, :, None]
    stiffness = omega_nat * omega_nat
    den_real = stiffness - omega_f * omega_f
    den_imag = 2.0 * damping[None, None, :, None] * omega_nat * omega_f
    magnitude = den_real * den_real + den_imag * den_imag
    return jnp.concatenate(
        [stiffness * den_real / magnitude, -stiffness * den_imag / magnitude], axis=0
    )


def oscillate_kernel(spec_ref, gain_ref, ce_ref, co_ref, se_ref, so_ref, wave_ref, peak_ref):
    step = pl.program_id(0)
    rows_per = peak_ref.shape[1]
    period_count, half = gain_ref.shape[2], gain_ref.shape[3]
    f32 = jnp.float32
    tables = (ce_ref, co_ref, se_ref, so_ref)

    @pl.when(step == 0)
    def _():
        parts = [
            jnp.dot(spec_ref[i // 2, i % 2].astype(jnp.bfloat16), tables[i][...], preferred_element_type=f32)
            for i in range(4)
        ]
        even, odd = parts[0] + parts[2], parts[1] + parts[3]
        wave_ref[:, : 2 * half] = even + odd
        wave_ref[:, 2 * half :] = even - odd

    stacked = [[], [], [], []]
    for r in range(rows_per):
        row = pl.ds(step * rows_per + r, 1)
        for parity in range(2):
            sr, si = spec_ref[0, parity, row, :], spec_ref[1, parity, row, :]
            gr, gi = gain_ref[0, parity], gain_ref[1, parity]
            stacked[parity].append((gr * sr - gi * si).astype(jnp.bfloat16))
            stacked[2 + parity].append((gr * si + gi * sr).astype(jnp.bfloat16))
    rows = [jnp.concatenate(group, axis=0) for group in stacked]
    ce, co, se, so = (
        jnp.dot(rows[i], tables[i][:, :half], preferred_element_type=f32) for i in range(4)
    )
    best = jnp.maximum(
        jnp.abs(ce + co) + jnp.abs(se + so), jnp.abs(ce - co) + jnp.abs(se - so)
    )
    best = jnp.max(best, axis=1, keepdims=True)
    lane = lax.broadcasted_iota(jnp.int32, (1, half), 1)
    signs = jnp.where(lane % 2 == 0, f32(1.0), f32(-1.0)) * f32(1.0 / math.sqrt(2 * half))
    middle = jnp.abs(jnp.sum(rows[0].astype(f32) * signs, axis=1, keepdims=True)) + jnp.abs(
        jnp.sum(rows[3].astype(f32) * signs, axis=1, keepdims=True)
    )
    best = jnp.maximum(best, middle)
    shape = (period_count, period_count)
    diag = lax.broadcasted_iota(jnp.int32, shape, 0) == lax.broadcasted_iota(jnp.int32, shape, 1)
    for r in range(rows_per):
        column = best[r * period_count : (r + 1) * period_count]
        peak_ref[0, r : r + 1, :] = jnp.sum(
            jnp.where(diag, column, f32(0.0)), axis=0, keepdims=True
        )


def oscillate(spectra, gain, tables):
    row_count, half = spectra.shape[2:]
    period_count = gain.shape[2]
    rows_per = math.gcd(row_count, 4)
    steps = row_count // rows_per
    whole = lambda shape: pl.BlockSpec(shape, lambda i: (0,) * len(shape), pipeline_mode=pl.Buffered(1))
    wave, peak = pl.pallas_call(
        oscillate_kernel,
        grid=(steps,),
        in_specs=[whole(spectra.shape), whole(gain.shape)] + [whole(t.shape) for t in tables],
        out_specs=[
            pl.BlockSpec((row_count, 4 * half), lambda i: (0, 0)),
            pl.BlockSpec((1, rows_per, period_count), lambda i: (i, 0, 0)),
        ],
        out_shape=[
            jax.ShapeDtypeStruct((row_count, 4 * half), jnp.float32),
            jax.ShapeDtypeStruct((steps, rows_per, period_count), jnp.float32),
        ],
        compiler_params=pltpu.CompilerParams(vmem_limit_bytes=40 << 20),
    )(spectra, gain, *tables)
    return wave, peak


def plane_width(fault_count):
    return 2 ** ((fault_count.bit_length() - 1) // 2)


def collect_kernel(planes, inner, in_ref, out_ref, near, held, far, near_send, near_recv, far_send, far_recv):
    mesh_type = pl.DeviceIdType.MESH
    f32 = jnp.float32
    group = out_ref.shape[0]
    members = inner * group
    fault, rup = lax.axis_index("fault"), lax.axis_index("rup")
    plane, place = fault // inner, fault % inner
    member = place * group + rup

    def mate(d):
        other = (member + d) % members
        return other, (plane * inner + other // group, other % group)

    def across(dz):
        other = (plane + dz) % planes
        return other, (other * inner + place, rup)

    barrier = pltpu.get_barrier_semaphore()
    for d in range(1, members):
        pl.semaphore_signal(barrier, inc=1, device_id=mate(d)[1], device_id_type=mesh_type)
    for dz in range(1, planes):
        pl.semaphore_signal(barrier, inc=1, device_id=across(dz)[1], device_id_type=mesh_type)
    pl.semaphore_wait(barrier, members + planes - 2)

    near_copies, far_copies = {}, {}
    for dz in range(1, planes + 1):
        target = (plane + dz) % planes
        for d in range(1, members):
            other, device = mate(d)
            near_copies[dz, d] = pltpu.make_async_remote_copy(
                src_ref=in_ref.at[target, other],
                dst_ref=near.at[dz - 1, d - 1],
                send_sem=near_send.at[dz - 1, d - 1],
                recv_sem=near_recv.at[dz - 1, d - 1],
                device_id=device,
                device_id_type=mesh_type,
            )
            near_copies[dz, d].start()
    for dz in range(1, planes + 1):
        target = (plane + dz) % planes
        for d in range(1, members):
            near_copies[dz, d].wait_recv()
        for k in range(group):
            terms = [near[dz - 1, d - 1].astype(f32) for d in range(1, members) if d % group == k]
            if k == 0:
                terms.append(in_ref[target, member].astype(f32))
            total = sum(terms[1:], terms[0])
            if dz < planes:
                held[dz - 1, k] = total.astype(held.dtype)
            else:
                out_ref[k] = total
        if dz < planes:
            far_copies[dz] = pltpu.make_async_remote_copy(
                src_ref=held.at[dz - 1],
                dst_ref=far.at[dz - 1],
                send_sem=far_send.at[dz - 1],
                recv_sem=far_recv.at[dz - 1],
                device_id=across(dz)[1],
                device_id_type=mesh_type,
            )
            far_copies[dz].start()
    for dz in range(1, planes):
        far_copies[dz].wait_recv()
        out_ref[...] += far[dz - 1].astype(f32)
    for copy in list(near_copies.values()) + list(far_copies.values()):
        copy.wait_send()


def collect(partial, fault_count, group):
    inner = plane_width(fault_count)
    planes, members = fault_count // inner, inner * group
    rows, width = partial.shape[1:]
    vmem = pl.BlockSpec(memory_space=pltpu.VMEM)
    dma = pltpu.SemaphoreType.DMA
    return pl.pallas_call(
        lambda *refs: collect_kernel(planes, inner, *refs),
        in_specs=[vmem],
        out_specs=vmem,
        out_shape=jax.ShapeDtypeStruct((group, rows, width), jnp.float32),
        scratch_shapes=[
            pltpu.VMEM((planes, members - 1, rows, width), partial.dtype),
            pltpu.VMEM((planes - 1, group, rows, width), partial.dtype),
            pltpu.VMEM((planes - 1, group, rows, width), partial.dtype),
            dma((planes, members - 1)),
            dma((planes, members - 1)),
            dma((planes - 1,)),
            dma((planes - 1,)),
        ],
        compiler_params=pltpu.CompilerParams(
            collective_id=0, has_side_effects=True, vmem_limit_bytes=16 << 20
        ),
    )(partial.reshape(planes, members, rows, width))


def body(green, slip_weights, slip_spectra, block_lists, block_counts, natural_freq, damping):
    fault_count = lax.axis_size("fault")
    group_size = lax.axis_size("rup")
    owned_count, slot_width = block_lists.shape
    blocks_local, points, terms, comp_count, _, freq_local = green.shape
    freq_count = slip_spectra.shape[3]
    inner_width = points * terms
    block_total = blocks_local * fault_count
    device_count = fault_count * group_size
    slot_rows = owned_count * slot_width
    axes = ("fault", "rup")
    bf16, f32 = jnp.bfloat16, jnp.float32
    slot_index = lax.broadcasted_iota(jnp.int32, (owned_count, slot_width), 1)
    named = jnp.where(slot_index < block_counts[:, None], block_lists, -1).reshape(1, slot_rows)
    pick_shape = (block_total, owned_count, slot_rows)
    row_block = lax.broadcasted_iota(jnp.int32, pick_shape, 0)
    row_owner = lax.broadcasted_iota(jnp.int32, pick_shape, 1)
    col_owner = lax.broadcasted_iota(jnp.int32, pick_shape, 2) // slot_width
    pick = ((named[None] == row_block) & (row_owner == col_owner)).astype(bf16)
    pick = pick.reshape(block_total * owned_count, slot_rows)
    from_index = jnp.arange(inner_width, dtype=jnp.int32)
    to_index = (from_index % points) * terms + from_index // points
    turn = (to_index[:, None] == from_index[None, :]).astype(bf16)
    weight_rows = slip_weights.transpose(0, 1, 3, 2).reshape(slot_rows, inner_width)
    weight_rows = jnp.dot(weight_rows, turn, preferred_element_type=f32).astype(bf16)
    weight_send = jnp.dot(pick, weight_rows, preferred_element_type=f32).astype(bf16)
    weight_send = weight_send.reshape(fault_count, blocks_local, owned_count, inner_width)
    weight_own = lax.all_to_all(weight_send, "fault", split_axis=0, concat_axis=0, tiled=True)
    rup = lax.axis_index("rup")
    weight_recv = [weight_own]
    for shift in range(1, group_size):
        ring = [(i, (i + shift) % group_size) for i in range(group_size)]
        weight_recv.append(lax.ppermute(weight_own, "rup", ring))
    slip_rows = slip_spectra.reshape(slot_rows, 2, group_size, freq_local).transpose(0, 2, 1, 3)
    slip_rows = slip_rows.reshape(slot_rows, 2 * freq_count)
    slip_send = jnp.dot(pick, slip_rows, preferred_element_type=f32).astype(bf16)
    slip_send = slip_send.reshape(
        fault_count, blocks_local, owned_count, group_size, 2, freq_local
    ).transpose(0, 3, 1, 4, 2, 5)
    slip_send = slip_send.reshape(device_count, blocks_local, 2, owned_count, freq_local)
    slip_recv = lax.all_to_all(slip_send, axes, split_axis=0, concat_axis=0, tiled=True)
    tile_mats = green.reshape(blocks_local, inner_width, comp_count * 2 * freq_local)
    weight_all = jnp.stack(
        [
            lax.select_n((rup - g) % group_size, *weight_recv)
            if group_size == 2
            else lax.dynamic_index_in_dim(
                jnp.stack(weight_recv), (rup - g) % group_size, 0, keepdims=False
            )
            for g in range(group_size)
        ],
        axis=1,
    ).reshape(device_count, blocks_local, owned_count, inner_width)
    product = jnp.einsum("sbqi,bix->sbqx", weight_all, tile_mats, preferred_element_type=f32)
    slip_f = slip_recv.astype(f32)
    ones = []
    for c in range(comp_count):
        at = 2 * c * freq_local
        prod_real = product[:, :, :, at : at + freq_local]
        prod_imag = product[:, :, :, at + freq_local : at + 2 * freq_local]
        slip_real, slip_imag = slip_f[:, :, 0], slip_f[:, :, 1]
        ones.append(jnp.sum(prod_real * slip_real - prod_imag * slip_imag, axis=1))
        ones.append(jnp.sum(prod_real * slip_imag + prod_imag * slip_real, axis=1))
    partial = jnp.stack([one.astype(bf16) for one in ones], axis=1)
    order = jnp.arange(freq_local, dtype=jnp.int32)
    split_to = (order % 2) * (freq_local // 2) + order // 2
    deal = (split_to[:, None] == order[None, :]).astype(bf16)
    partial = jnp.dot(
        partial.reshape(device_count * comp_count * 2 * owned_count, freq_local),
        deal,
        preferred_element_type=f32,
    ).astype(bf16)
    partial = partial.reshape(device_count, comp_count * 2 * owned_count, freq_local)
    shares = collect(partial, fault_count, group_size)
    shares = jnp.stack(
        [
            lax.select_n((rup - g) % group_size, shares[0], shares[1])
            if group_size == 2
            else lax.dynamic_index_in_dim(shares, (rup - g) % group_size, 0, keepdims=False)
            for g in range(group_size)
        ]
    )
    shares = shares.reshape(group_size, comp_count, 2, owned_count, 2, freq_local // 2)
    spectra = shares.transpose(2, 4, 1, 3, 0, 5)
    spectra = spectra.reshape(2, 2, comp_count * owned_count, freq_count // 2)
    gain = split_gain(natural_freq, damping, freq_count)
    tables = half_tables(freq_count)
    wave, peak = oscillate(spectra, gain, tables)
    period_count = natural_freq.shape[0]
    waveform = wave.reshape(comp_count, owned_count, 2 * freq_count).transpose(1, 0, 2)
    peaks = peak.reshape(comp_count, owned_count, period_count).transpose(1, 0, 2)
    return (waveform, peaks)


def solution(mesh):
    return jax.shard_map(
        body,
        mesh=mesh,
        in_specs=(
            P("fault", None, None, None, None, "rup"),
            P(("fault", "rup"), None, None, None),
            P(("fault", "rup"), None, None, None),
            P(("fault", "rup"), None),
            P(("fault", "rup")),
            P(),
            P(),
        ),
        out_specs=(P(("fault", "rup"), None, None), P(("fault", "rup"), None, None)),
        check_vma=False,
    )
```

```python
import math

import jax
import jax.numpy as jnp
from jax import lax
from jax.experimental import pallas as pl
from jax.experimental.pallas import tpu as pltpu
from jax.sharding import PartitionSpec as P

LANES = 128


def phase_waves(freq_index, time_index, sample_count):
    phase = freq_index[:, None] * time_index[None, :] % sample_count
    angle = phase.astype(jnp.float32) * jnp.float32(2.0 * math.pi / sample_count)
    return jnp.cos(angle), jnp.sin(angle)


def half_tables(freq_count):
    sample_count = 2 * freq_count
    scale = jnp.float32(1.0 / math.sqrt(freq_count))
    fine = jnp.arange(LANES, dtype=jnp.int32)
    coarse = jnp.arange(freq_count // LANES, dtype=jnp.int32) * LANES
    cosines, sines = [], []
    for parity in range(2):
        freq_index = 2 * jnp.arange(freq_count // 2, dtype=jnp.int32) + parity
        cos_f, sin_f = phase_waves(freq_index, fine, sample_count)
        cos_c, sin_c = phase_waves(freq_index, coarse, sample_count)
        cos_f, sin_f, cos_c, sin_c = lax.optimization_barrier(
            (cos_f * scale, sin_f * scale, cos_c, sin_c)
        )
        cos_parts, sin_parts = [], []
        for a in range(freq_count // LANES):
            ca, sa = cos_c[:, a : a + 1], sin_c[:, a : a + 1]
            cos_parts.append((ca * cos_f - sa * sin_f).astype(jnp.bfloat16))
            sin_parts.append((-(sa * cos_f + ca * sin_f)).astype(jnp.bfloat16))
        cosines.append(jnp.concatenate(cos_parts, axis=1))
        sines.append(jnp.concatenate(sin_parts, axis=1))
    return (cosines[0], cosines[1], sines[0], sines[1])


def split_gain(natural_freq, damping, freq_count):
    freq_index = jnp.arange(freq_count, dtype=jnp.float32).reshape(freq_count // 2, 2).T
    freq_index = freq_index.reshape(1, 2, 1, freq_count // 2)
    omega_f = freq_index * jnp.float32(math.pi / freq_count)
    omega_nat = (jnp.float32(math.pi) * natural_freq)[None, None, :, None]
    stiffness = omega_nat * omega_nat
    den_real = stiffness - omega_f * omega_f
    den_imag = 2.0 * damping[None, None, :, None] * omega_nat * omega_f
    magnitude = den_real * den_real + den_imag * den_imag
    return jnp.concatenate(
        [stiffness * den_real / magnitude, -stiffness * den_imag / magnitude], axis=0
    )


def oscillate_kernel(spec_ref, gain_ref, ce_ref, co_ref, se_ref, so_ref, wave_ref, peak_ref):
    step = pl.program_id(0)
    rows_per = peak_ref.shape[1]
    period_count, half = gain_ref.shape[2], gain_ref.shape[3]
    f32 = jnp.float32
    tables = (ce_ref, co_ref, se_ref, so_ref)

    @pl.when(step == 0)
    def _():
        parts = [
            jnp.dot(spec_ref[i // 2, i % 2].astype(jnp.bfloat16), tables[i][...], preferred_element_type=f32)
            for i in range(4)
        ]
        even, odd = parts[0] + parts[2], parts[1] + parts[3]
        wave_ref[:, : 2 * half] = even + odd
        wave_ref[:, 2 * half :] = even - odd

    stacked = [[], [], [], []]
    for r in range(rows_per):
        row = pl.ds(step * rows_per + r, 1)
        for parity in range(2):
            sr, si = spec_ref[0, parity, row, :], spec_ref[1, parity, row, :]
            gr, gi = gain_ref[0, parity], gain_ref[1, parity]
            stacked[parity].append((gr * sr - gi * si).astype(jnp.bfloat16))
            stacked[2 + parity].append((gr * si + gi * sr).astype(jnp.bfloat16))
    rows = [jnp.concatenate(group, axis=0) for group in stacked]
    ce, co, se, so = (
        jnp.dot(rows[i], tables[i][:, :half], preferred_element_type=f32) for i in range(4)
    )
    best = jnp.maximum(
        jnp.abs(ce + co) + jnp.abs(se + so), jnp.abs(ce - co) + jnp.abs(se - so)
    )
    best = jnp.max(best, axis=1, keepdims=True)
    lane = lax.broadcasted_iota(jnp.int32, (1, half), 1)
    signs = jnp.where(lane % 2 == 0, f32(1.0), f32(-1.0)) * f32(1.0 / math.sqrt(2 * half))
    middle = jnp.abs(jnp.sum(rows[0].astype(f32) * signs, axis=1, keepdims=True)) + jnp.abs(
        jnp.sum(rows[3].astype(f32) * signs, axis=1, keepdims=True)
    )
    best = jnp.maximum(best, middle)
    shape = (period_count, period_count)
    diag = lax.broadcasted_iota(jnp.int32, shape, 0) == lax.broadcasted_iota(jnp.int32, shape, 1)
    for r in range(rows_per):
        column = best[r * period_count : (r + 1) * period_count]
        peak_ref[0, r : r + 1, :] = jnp.sum(
            jnp.where(diag, column, f32(0.0)), axis=0, keepdims=True
        )


def oscillate(spectra, gain, tables):
    row_count, half = spectra.shape[2:]
    period_count = gain.shape[2]
    rows_per = math.gcd(row_count, 8)
    steps = row_count // rows_per
    whole = lambda shape: pl.BlockSpec(shape, lambda i: (0,) * len(shape), pipeline_mode=pl.Buffered(1))
    wave, peak = pl.pallas_call(
        oscillate_kernel,
        grid=(steps,),
        in_specs=[whole(spectra.shape), whole(gain.shape)] + [whole(t.shape) for t in tables],
        out_specs=[
            pl.BlockSpec((row_count, 4 * half), lambda i: (0, 0)),
            pl.BlockSpec((1, rows_per, period_count), lambda i: (i, 0, 0)),
        ],
        out_shape=[
            jax.ShapeDtypeStruct((row_count, 4 * half), jnp.float32),
            jax.ShapeDtypeStruct((steps, rows_per, period_count), jnp.float32),
        ],
        compiler_params=pltpu.CompilerParams(vmem_limit_bytes=40 << 20),
    )(spectra, gain, *tables)
    return wave, peak


def plane_width(fault_count):
    return 2 ** ((fault_count.bit_length() - 1) // 2)


def collect_kernel(planes, inner, in_ref, out_ref, near, held, far, near_send, near_recv, far_send, far_recv):
    mesh_type = pl.DeviceIdType.MESH
    f32 = jnp.float32
    group = out_ref.shape[0]
    members = inner * group
    fault, rup = lax.axis_index("fault"), lax.axis_index("rup")
    plane, place = fault // inner, fault % inner
    member = place * group + rup

    def mate(d):
        other = (member + d) % members
        return other, (plane * inner + other // group, other % group)

    def across(dz):
        other = (plane + dz) % planes
        return other, (other * inner + place, rup)

    barrier = pltpu.get_barrier_semaphore()
    for d in range(1, members):
        pl.semaphore_signal(barrier, inc=1, device_id=mate(d)[1], device_id_type=mesh_type)
    for dz in range(1, planes):
        pl.semaphore_signal(barrier, inc=1, device_id=across(dz)[1], device_id_type=mesh_type)
    pl.semaphore_wait(barrier, members + planes - 2)

    near_copies, far_copies = {}, {}
    for dz in range(1, planes + 1):
        target = (plane + dz) % planes
        for d in range(1, members):
            other, device = mate(d)
            near_copies[dz, d] = pltpu.make_async_remote_copy(
                src_ref=in_ref.at[target, other],
                dst_ref=near.at[dz - 1, d - 1],
                send_sem=near_send.at[dz - 1, d - 1],
                recv_sem=near_recv.at[dz - 1, d - 1],
                device_id=device,
                device_id_type=mesh_type,
            )
            near_copies[dz, d].start()
    for dz in range(1, planes + 1):
        target = (plane + dz) % planes
        for d in range(1, members):
            near_copies[dz, d].wait_recv()
        for k in range(group):
            terms = [near[dz - 1, d - 1].astype(f32) for d in range(1, members) if d % group == k]
            if k == 0:
                terms.append(in_ref[target, member].astype(f32))
            total = sum(terms[1:], terms[0])
            if dz < planes:
                held[dz - 1, k] = total.astype(held.dtype)
            else:
                out_ref[k] = total
        if dz < planes:
            far_copies[dz] = pltpu.make_async_remote_copy(
                src_ref=held.at[dz - 1],
                dst_ref=far.at[dz - 1],
                send_sem=far_send.at[dz - 1],
                recv_sem=far_recv.at[dz - 1],
                device_id=across(dz)[1],
                device_id_type=mesh_type,
            )
            far_copies[dz].start()
    for dz in range(1, planes):
        far_copies[dz].wait_recv()
        out_ref[...] += far[dz - 1].astype(f32)
    for copy in list(near_copies.values()) + list(far_copies.values()):
        copy.wait_send()


def collect(partial, fault_count, group):
    inner = plane_width(fault_count)
    planes, members = fault_count // inner, inner * group
    rows, width = partial.shape[1:]
    vmem = pl.BlockSpec(memory_space=pltpu.VMEM)
    dma = pltpu.SemaphoreType.DMA
    return pl.pallas_call(
        lambda *refs: collect_kernel(planes, inner, *refs),
        in_specs=[vmem],
        out_specs=vmem,
        out_shape=jax.ShapeDtypeStruct((group, rows, width), jnp.float32),
        scratch_shapes=[
            pltpu.VMEM((planes, members - 1, rows, width), partial.dtype),
            pltpu.VMEM((planes - 1, group, rows, width), partial.dtype),
            pltpu.VMEM((planes - 1, group, rows, width), partial.dtype),
            dma((planes, members - 1)),
            dma((planes, members - 1)),
            dma((planes - 1,)),
            dma((planes - 1,)),
        ],
        compiler_params=pltpu.CompilerParams(
            collective_id=0, has_side_effects=True, vmem_limit_bytes=16 << 20
        ),
    )(partial.reshape(planes, members, rows, width))


def body(green, slip_weights, slip_spectra, block_lists, block_counts, natural_freq, damping):
    fault_count = lax.axis_size("fault")
    group_size = lax.axis_size("rup")
    owned_count, slot_width = block_lists.shape
    blocks_local, points, terms, comp_count, _, freq_local = green.shape
    freq_count = slip_spectra.shape[3]
    inner_width = points * terms
    block_total = blocks_local * fault_count
    device_count = fault_count * group_size
    slot_rows = owned_count * slot_width
    axes = ("fault", "rup")
    bf16, f32 = jnp.bfloat16, jnp.float32
    slot_index = lax.broadcasted_iota(jnp.int32, (owned_count, slot_width), 1)
    named = jnp.where(slot_index < block_counts[:, None], block_lists, -1).reshape(1, slot_rows)
    pick_shape = (block_total, owned_count, slot_rows)
    row_block = lax.broadcasted_iota(jnp.int32, pick_shape, 0)
    row_owner = lax.broadcasted_iota(jnp.int32, pick_shape, 1)
    col_owner = lax.broadcasted_iota(jnp.int32, pick_shape, 2) // slot_width
    pick = ((named[None] == row_block) & (row_owner == col_owner)).astype(bf16)
    pick = pick.reshape(block_total * owned_count, slot_rows)
    from_index = jnp.arange(inner_width, dtype=jnp.int32)
    to_index = (from_index % points) * terms + from_index // points
    turn = (to_index[:, None] == from_index[None, :]).astype(bf16)
    weight_rows = slip_weights.transpose(0, 1, 3, 2).reshape(slot_rows, inner_width)
    weight_rows = jnp.dot(weight_rows, turn, preferred_element_type=f32).astype(bf16)
    weight_send = jnp.dot(pick, weight_rows, preferred_element_type=f32).astype(bf16)
    weight_send = weight_send.reshape(fault_count, blocks_local, owned_count, inner_width)
    weight_own = lax.all_to_all(weight_send, "fault", split_axis=0, concat_axis=0, tiled=True)
    rup = lax.axis_index("rup")
    weight_recv = [weight_own]
    for shift in range(1, group_size):
        ring = [(i, (i + shift) % group_size) for i in range(group_size)]
        weight_recv.append(lax.ppermute(weight_own, "rup", ring))
    slip_rows = slip_spectra.reshape(slot_rows, 2, group_size, freq_local).transpose(0, 2, 1, 3)
    slip_rows = slip_rows.reshape(slot_rows, 2 * freq_count)
    slip_send = jnp.dot(pick, slip_rows, preferred_element_type=f32).astype(bf16)
    slip_send = slip_send.reshape(
        fault_count, blocks_local, owned_count, group_size, 2, freq_local
    ).transpose(0, 3, 1, 4, 2, 5)
    slip_send = slip_send.reshape(device_count, blocks_local, 2, owned_count, freq_local)
    slip_recv = lax.all_to_all(slip_send, axes, split_axis=0, concat_axis=0, tiled=True)
    tile_mats = green.reshape(blocks_local, inner_width, comp_count * 2 * freq_local)
    weight_all = jnp.stack(
        [
            lax.select_n((rup - g) % group_size, *weight_recv)
            if group_size == 2
            else lax.dynamic_index_in_dim(
                jnp.stack(weight_recv), (rup - g) % group_size, 0, keepdims=False
            )
            for g in range(group_size)
        ],
        axis=1,
    ).reshape(device_count, blocks_local, owned_count, inner_width)
    product = jnp.einsum("sbqi,bix->sbqx", weight_all, tile_mats, preferred_element_type=f32)
    slip_f = slip_recv.astype(f32)
    ones = []
    for c in range(comp_count):
        at = 2 * c * freq_local
        prod_real = product[:, :, :, at : at + freq_local]
        prod_imag = product[:, :, :, at + freq_local : at + 2 * freq_local]
        slip_real, slip_imag = slip_f[:, :, 0], slip_f[:, :, 1]
        ones.append(jnp.sum(prod_real * slip_real - prod_imag * slip_imag, axis=1))
        ones.append(jnp.sum(prod_real * slip_imag + prod_imag * slip_real, axis=1))
    partial = jnp.stack([one.astype(bf16) for one in ones], axis=1)
    order = jnp.arange(freq_local, dtype=jnp.int32)
    split_to = (order % 2) * (freq_local // 2) + order // 2
    deal = (split_to[:, None] == order[None, :]).astype(bf16)
    partial = jnp.dot(
        partial.reshape(device_count * comp_count * 2 * owned_count, freq_local),
        deal,
        preferred_element_type=f32,
    ).astype(bf16)
    partial = partial.reshape(device_count, comp_count * 2 * owned_count, freq_local)
    shares = collect(partial, fault_count, group_size)
    shares = jnp.stack(
        [
            lax.select_n((rup - g) % group_size, shares[0], shares[1])
            if group_size == 2
            else lax.dynamic_index_in_dim(shares, (rup - g) % group_size, 0, keepdims=False)
            for g in range(group_size)
        ]
    )
    shares = shares.reshape(group_size, comp_count, 2, owned_count, 2, freq_local // 2)
    spectra = shares.transpose(2, 4, 1, 3, 0, 5)
    spectra = spectra.reshape(2, 2, comp_count * owned_count, freq_count // 2)
    gain = split_gain(natural_freq, damping, freq_count)
    tables = half_tables(freq_count)
    wave, peak = oscillate(spectra, gain, tables)
    period_count = natural_freq.shape[0]
    waveform = wave.reshape(comp_count, owned_count, 2 * freq_count).transpose(1, 0, 2)
    peaks = peak.reshape(comp_count, owned_count, period_count).transpose(1, 0, 2)
    return (waveform, peaks)


def solution(mesh):
    return jax.shard_map(
        body,
        mesh=mesh,
        in_specs=(
            P("fault", None, None, None, None, "rup"),
            P(("fault", "rup"), None, None, None),
            P(("fault", "rup"), None, None, None),
            P(("fault", "rup"), None),
            P(("fault", "rup")),
            P(),
            P(),
        ),
        out_specs=(P(("fault", "rup"), None, None), P(("fault", "rup"), None, None)),
        check_vma=False,
    )
```
